32 devices in a mesh: batch: 2 (over y), freq: 8 (over z, x), elem: 2 (over core).
Axes of the slice: x: 2, y: 2, z: 4, core: 2. Of those that a mesh axis runs over, the one named last changes fastest.
Arguments:
- flaw_cells: int32 [512], P('batch'), parts along dimension 0, may hold values from 0 to 255, each once
- flaw_blocks: int32 [16], P('batch'), parts along dimension 0, may hold values from 0 to 7, each once
- element_channel: int32 [256], P('elem'), may hold values from 0 to 255, each once
- focal_delay: float32 [256, 256], replicated, may hold values from 0 to 64
- beam_field: bfloat16 [128, 2, 256, 256], P('freq', None, 'elem'), may hold values from -0.125 to 0.125
- flaw_size: float32 [4, 128], P('batch'), parts along dimension 0, may hold values from 0.5 to 4
- flaw_slope: float32 [4, 128], P('batch'), parts along dimension 0, may hold values from 0.2 to 1
- noise_level: float32 [4, 128], P(('batch', 'elem'), 'freq'), parts along dimension 0, may hold values from 0.5 to 5
Outputs:
- flaw_peak: float32 [4, 128], P(('batch', 'elem'), 'freq'), parts along dimension 0
- detection: float32 [4, 128], P(('batch', 'elem'), 'freq'), parts along dimension 0
The draws below stay inside these ranges and needn't reach their ends.
There are 2 independent parts, one for each index of `batch`. The reference program is written for one: setup_inputs(seed, part) draws one part's arguments, and reference() takes and returns one part's arrays. A program takes and returns all parts, laid end to end along the dimension named above; an argument that names none is the same for every part. Nothing has to cross between parts.
Inputs may be any that keep to these rules, and one draw needn't show every extreme that they name: `flaw_cells`: every site holds exactly one flaw. `flaw_blocks`: every scan block belongs to exactly one flaw group. `element_channel`: every channel drives exactly one element.
All inputs are finite; a program needn't handle non-finite values.
Results may differ from the reference program's by a relative error of at most 0.0011.
Values may be sent and summed in bfloat16 or wider, within the bound.
A program may use at most 64 MiB of HBM per device.

```python
import math
import jax
import jax.numpy as jnp
from jax import lax

W_DEV = 16
NW = 128
E = 256
E_GRP = 128
FG = 128
NG = 2
NB = 4
SB = 32
NSB = 8
S = 256
CELLS = 256
NT = 256
N_ELEM = 2


def levels(stream_key, dims, pieces, least, top_value):
    factor_of, own = 1.0, jax.random.fold_in(stream_key, 6)
    for position, blocks in pieces:
        draws = jnp.exp(jax.random.uniform(jax.random.fold_in(own, position), (blocks,), jnp.float32, least / len(pieces), top_value / len(pieces)))
        factor_of = factor_of * jnp.repeat(draws, dims[position] // blocks).reshape([-1 if axis == position else 1 for axis in range(len(dims))])
    return factor_of


def gaussian(own_key, shape, spread, most, shards=(), kind=jnp.bfloat16):
    entries = jax.random.normal(own_key, shape, jnp.float32) * spread
    if len(shards) > 0:
        entries = levels(own_key, shape, shards, -0.22, 0.18) * entries
    return jnp.clip(entries, min=-most, max=most).astype(kind)


def setup_inputs(seed: int = 0, part: int = 0) -> dict:
    key_of = jax.random.split(jax.random.key(seed), 9)
    own_keys = jax.random.split(jax.random.fold_in(key_of[8], part), 9)
    return {
        "flaw_cells": jax.random.permutation(own_keys[0], CELLS).astype(jnp.int32),
        "flaw_blocks": jax.random.permutation(own_keys[1], NSB).astype(jnp.int32),
        "element_channel": jax.random.permutation(key_of[2], E).astype(jnp.int32),
        "focal_delay": jnp.clip(jax.random.uniform(key_of[3], (E, S), jnp.float32, 0.0, 64.0), 0.0, 64.0),
        "beam_field": gaussian(key_of[4], (NW, 2, E, CELLS), (8 * E) ** -0.5, 0.125, ((0, 8), (2, 2))),
        "flaw_size": jnp.clip(jnp.exp(jax.random.uniform(own_keys[5], (NG, FG), jnp.float32, math.log(0.5), math.log(4.0))), 0.5, 4.0),
        "flaw_slope": jnp.clip(jax.random.uniform(own_keys[6], (NG, FG), jnp.float32, 0.2, 1.0), 0.2, 1.0),
        "noise_level": jnp.clip(jnp.exp(math.log(5.0) - 2.3025851 * jax.random.uniform(own_keys[7], (NG, FG), jnp.float32) ** levels(own_keys[7], (NG, FG), ((0, 2), (1, 8)), -0.2, 0.2)), 0.5, 5.0),
    }


EDGE = 0.6
STEEP = 3.0
EPS = 1e-05

def kirchhoff(angular, flaw_size, flaw_slope):
    angles = angular[None, :, None] * (2.0 * flaw_size * flaw_slope)[:, None, :]
    real_part = flaw_size[:, None, :] * (1.0 + EDGE) * jnp.cos(angles)
    imag_part = flaw_size[:, None, :] * (EDGE - 1.0) * jnp.sin(angles)
    return (real_part, imag_part)

def focal_law(angular, delays):
    phases = angular[:, None, None, None] * delays[None]
    return jnp.concatenate([jnp.cos(phases), -jnp.sin(phases)], axis=-1).astype(jnp.bfloat16)

def field_matrix(fields):
    real_part = fields[:, 0]
    imag_part = fields[:, 1]
    upper_rows = jnp.concatenate([real_part, imag_part], axis=-1)
    lower_rows = jnp.concatenate([-imag_part, real_part], axis=-1)
    return jnp.concatenate([upper_rows, lower_rows], axis=1)

def combine(product, k_real, k_imag):
    columns = k_real.shape[-1]
    real_part = product[..., :columns]
    imag_part = product[..., columns:]
    scale_real = k_real[:, :, None, :]
    scale_imag = k_imag[:, :, None, :]
    return jnp.stack([scale_real * real_part - scale_imag * imag_part, scale_real * imag_part + scale_imag * real_part], axis=2)

def reference(flaw_cells, flaw_blocks, element_channel, focal_delay, beam_field, flaw_size, flaw_slope, noise_level):
    row_total = NB * SB
    scan_rows = (flaw_blocks.reshape(NG, NB)[:, :, None] * SB + jnp.arange(SB, dtype=jnp.int32)[None, None, :]).reshape(NG, row_total)
    delays = jnp.moveaxis(jnp.take(jnp.take(focal_delay, element_channel, axis=0), scan_rows, axis=1), 0, 2)

    def one_block(starts):
        freq_index = starts + jnp.arange(W_DEV, dtype=jnp.int32)
        angular = freq_index.astype(jnp.float32) * (math.pi / NW)
        k_real, k_imag = kirchhoff(angular, flaw_size, flaw_slope)
        beam_block = lax.dynamic_slice_in_dim(beam_field, starts, W_DEV, 0)
        fields = jnp.take(beam_block, flaw_cells, axis=3).reshape(W_DEV, 2, E, NG, FG)
        summed = jnp.zeros((NG, W_DEV, 2, row_total, FG), jnp.float32)
        for member in range(N_ELEM):
            offset = member * E_GRP
            focal_terms = focal_law(angular, delays[:, :, offset:offset + E_GRP])
            field_terms = field_matrix(fields[:, :, offset:offset + E_GRP])
            product = jnp.einsum('wgre,wegf->gwrf', focal_terms.astype(jnp.float32), field_terms.astype(jnp.float32))
            partial_value = combine(product, k_real, k_imag).astype(jnp.bfloat16)
            summed = summed + partial_value.astype(jnp.float32)
        return summed.astype(jnp.bfloat16)
    block_starts = jnp.arange(NW // W_DEV, dtype=jnp.int32) * W_DEV
    spectra = lax.map(one_block, block_starts)

    def envelope(group_spectra):
        values = group_spectra.reshape(NW, 2, row_total, FG).astype(jnp.float32)
        signal = lax.complex(values[:, 0], values[:, 1])
        padded = jnp.concatenate([signal, jnp.zeros_like(signal)], axis=0)
        in_time = jnp.fft.ifft(padded, axis=0)[:NT] * (2.0 * NW / math.sqrt(NW))
        return lax.optimization_barrier(jnp.max(jnp.abs(in_time), axis=(0, 1)))
    flaw_peak = lax.map(envelope, jnp.moveaxis(spectra, 1, 0))
    detection = jax.nn.sigmoid(STEEP * (jnp.log(flaw_peak + EPS) - jnp.log(noise_level)))
    return (flaw_peak, detection)
```

```python
import functools
import math

import jax
import jax.numpy as jnp
import numpy as np
from jax import lax
from jax.experimental import pallas as pl
from jax.experimental.pallas import tpu as pltpu
from jax.sharding import PartitionSpec as P

W_DEV = 16
FG = 128
NB = 4
SB = 32
T_CAP = 1024


EDGE = 0.6
STEEP = 3.0
EPS = 1e-05


def kirchhoff(angular, flaw_size, flaw_slope):
    angles = angular[None, :, None] * (2.0 * flaw_size * flaw_slope)[:, None, :]
    real_part = flaw_size[:, None, :] * (1.0 + EDGE) * jnp.cos(angles)
    imag_part = flaw_size[:, None, :] * (EDGE - 1.0) * jnp.sin(angles)
    return (real_part, imag_part)


def focal_law(angular, delays):
    phases = angular[:, None, None, None] * delays[None]
    return jnp.concatenate([jnp.cos(phases), -jnp.sin(phases)], axis=-1).astype(jnp.bfloat16)


def field_matrix(fields):
    real_part = fields[:, 0]
    imag_part = fields[:, 1]
    upper_rows = jnp.concatenate([real_part, imag_part], axis=-1)
    lower_rows = jnp.concatenate([-imag_part, real_part], axis=-1)
    return jnp.concatenate([upper_rows, lower_rows], axis=1)


def combine(product, k_real, k_imag):
    columns = k_real.shape[-1]
    real_part = product[..., :columns]
    imag_part = product[..., columns:]
    scale_real = k_real[:, :, None, :]
    scale_imag = k_imag[:, :, None, :]
    return jnp.stack(
        [
            scale_real * real_part - scale_imag * imag_part,
            scale_real * imag_part + scale_imag * real_part,
        ],
        axis=2,
    )


def envelope_peak(spectra, row_count):
    groups, freq_total, planes, columns = spectra.shape
    sample_count = min(T_CAP, 2 * freq_total)
    time_block = min(128, sample_count)
    freq_index = jnp.arange(freq_total, dtype=jnp.int32)
    scaling = 1.0 / math.sqrt(freq_total)

    def advance(step_index, running):
        sample_times = step_index * time_block + jnp.arange(time_block, dtype=jnp.int32)
        phase_steps = freq_index[:, None] * sample_times[None, :] % (2 * freq_total)
        angles = phase_steps.astype(jnp.float32) * (math.pi / freq_total)
        cosine = jnp.cos(angles)
        sine_part = jnp.sin(angles)
        twiddle = jnp.stack(
            [jnp.stack([cosine, sine_part], axis=1), jnp.stack([-sine_part, cosine], axis=1)],
            axis=1,
        )
        twiddle_high = lax.optimization_barrier(twiddle.astype(jnp.bfloat16))
        twiddle_low = (twiddle - twiddle_high.astype(jnp.float32)).astype(jnp.bfloat16)
        signal = jnp.einsum(
            "gwcx,wckt->gkxt", spectra, twiddle_high, preferred_element_type=jnp.float32
        )
        signal = signal + jnp.einsum(
            "gwcx,wckt->gkxt", spectra, twiddle_low, preferred_element_type=jnp.float32
        )
        signal = signal * scaling
        magnitude = jnp.sqrt(signal[:, 0] * signal[:, 0] + signal[:, 1] * signal[:, 1])
        magnitude = magnitude.reshape(groups, row_count, columns // row_count, time_block)
        return jnp.maximum(running, jnp.max(magnitude, axis=(1, 3)))

    initial = jnp.zeros((groups, columns // row_count), jnp.float32)
    return lax.fori_loop(0, sample_count // time_block, advance, initial)


def regroup_peaks(moved):
    groups, freq_total, planes, row_count, flaw_count = moved.shape
    return envelope_peak(
        moved.reshape(groups, freq_total, planes, row_count * flaw_count), row_count
    )


MESH = pl.DeviceIdType.MESH
HALF = W_DEV // 2
TILE_ROWS = 2 * HALF
NT_DIMS = (((1,), (1,)), ((), ()))


def dot_rows(left, right):
    return lax.dot_general(left, right, NT_DIMS, preferred_element_type=jnp.float32)


def unit_phasor(turns):
    rest = turns - jnp.floor(turns + 0.5)
    angle = rest * math.pi
    square = angle * angle
    sine = jnp.full_like(angle, -1.0 / math.factorial(11))
    for order, sign in ((9, 1.0), (7, -1.0), (5, 1.0), (3, -1.0), (1, 1.0)):
        sine = sine * square + sign / math.factorial(order)
    sine = sine * angle
    cosine = jnp.full_like(angle, 1.0 / math.factorial(12))
    for order, sign in ((10, -1.0), (8, 1.0), (6, -1.0), (4, 1.0), (2, -1.0), (0, 1.0)):
        cosine = cosine * square + sign / math.factorial(order)
    return 1.0 - 2.0 * sine * sine, -2.0 * sine * cosine


def half_twiddles(freq_count):
    freq_total = W_DEV * freq_count
    samples = np.arange(freq_total)
    halves = []
    for parity in range(2):
        freqs = (np.arange(freq_count)[:, None] * W_DEV + 2 * np.arange(HALF)[None, :] + parity).reshape(-1)
        angles = (samples[:, None] * freqs[None, :] % (2 * freq_total)) * (np.pi / freq_total)
        cosine, sine = np.cos(angles), np.sin(angles)
        real_rows = np.stack([cosine, -sine], axis=-1).reshape(freq_total, -1)
        imag_rows = np.stack([sine, cosine], axis=-1).reshape(freq_total, -1)
        whole = np.concatenate([real_rows, imag_rows], axis=0).astype(np.float32)
        high = whole.astype(jnp.bfloat16)
        low = (whole - high.astype(np.float32)).astype(jnp.bfloat16)
        halves.append(np.concatenate([high, low], axis=1))
    return np.stack(halves)


def inspect_kernel(
    freq_count,
    blocks_ref,
    cells_ref,
    channel_ref,
    delay_ref,
    field_hbm,
    size_ref,
    slope_ref,
    noise_ref,
    twiddle_ref,
    peak_ref,
    detection_ref,
    field_ref,
    select_ref,
    theta_ref,
    amp_ref,
    phase_ref,
    turn_ref,
    stage_ref,
    own_ref,
    give_ref,
    take_ref,
    spec_ref,
    recv_ref,
    even_ref,
    top_ref,
    field_sem,
    give_sem,
    take_sem,
    send_sem,
    recv_sem,
):
    freq_total = W_DEV * freq_count
    columns = FG // freq_count
    chunk = columns * TILE_ROWS
    me = lax.axis_index("freq")
    mine = lax.axis_index("elem")
    sibling = 1 - mine

    loads = [
        pltpu.make_async_copy(field_hbm.at[:, parity], field_ref.at[parity], field_sem.at[parity])
        for parity in range(2)
    ]
    for load in loads:
        load.start()

    barrier = pltpu.get_barrier_semaphore()
    pl.semaphore_signal(barrier, inc=1, device_id={"elem": sibling}, device_id_type=MESH)
    for step in range(1, freq_count):
        pl.semaphore_signal(
            barrier, inc=1, device_id={"freq": lax.rem(me + step, freq_count)}, device_id_type=MESH
        )

    cell_count = cells_ref.shape[1]
    cell_rows = lax.broadcasted_iota(jnp.int32, (cell_count, cell_count), 0)
    chosen = jnp.where(cell_rows == cells_ref[...], 1.0, 0.0)
    select_ref[...] = jnp.transpose(chosen).astype(jnp.bfloat16)

    channel_count, scan_count = delay_ref.shape
    element_count = channel_ref.shape[1]
    channel_rows = lax.broadcasted_iota(jnp.int32, (channel_count, element_count), 0)
    drives = jnp.transpose(jnp.where(channel_rows == channel_ref[...], 1.0, 0.0)).astype(jnp.bfloat16)
    sub = lax.broadcasted_iota(jnp.int32, (SB, scan_count), 0)
    lane = lax.broadcasted_iota(jnp.int32, (SB, scan_count), 1)
    rows = jnp.concatenate(
        [jnp.where(lane == sub + blocks_ref[j] * SB, 1.0, 0.0) for j in range(2 * NB)], axis=0
    ).astype(jnp.bfloat16)
    rest = delay_ref[...]
    delays = jnp.zeros((2 * FG, element_count), jnp.float32)
    for _ in range(3):
        piece = rest.astype(jnp.bfloat16)
        rest = rest - piece.astype(jnp.float32)
        by_element = jnp.dot(drives, piece, preferred_element_type=jnp.float32).astype(jnp.bfloat16)
        delays = delays + dot_rows(rows, by_element)
    theta_ref[: 2 * FG] = delays
    for group in range(2):
        size = jnp.transpose(jnp.broadcast_to(size_ref[group : group + 1, :], (FG, FG)))
        slope = jnp.transpose(jnp.broadcast_to(slope_ref[group : group + 1, :], (FG, FG)))
        theta_ref[(2 + group) * FG : (3 + group) * FG] = 2.0 * size * slope
        amp_ref[group * FG : (group + 1) * FG] = size
    scale = 0.5 / freq_total
    turn_real, turn_imag = unit_phasor(theta_ref[...] * (2.0 * scale))
    turn_ref[0] = turn_real
    turn_ref[1] = turn_imag

    def group_spectra(parity, group):
        base = pl.multiple_of(group * FG, FG)
        tail = pl.multiple_of((2 + group) * FG, FG)

        def one_freq(index, carry):
            focal_real = phase_ref[0, pl.ds(base, FG), :]
            focal_imag = phase_ref[1, pl.ds(base, FG), :]
            fields = dot_rows(select_ref[pl.ds(base, FG), :], field_ref[parity, index])
            weights = jnp.concatenate(
                [
                    jnp.concatenate([focal_real, -focal_imag], axis=1),
                    jnp.concatenate([focal_imag, focal_real], axis=1),
                ],
                axis=0,
            ).astype(jnp.bfloat16)
            product = dot_rows(fields.astype(jnp.bfloat16), weights)
            real_part = product[:, :FG]
            imag_part = product[:, FG:]
            edge_real = phase_ref[0, pl.ds(tail, FG), :]
            edge_imag = phase_ref[1, pl.ds(tail, FG), :]
            amp = amp_ref[pl.ds(base, FG), :]
            k_real = amp * (1.0 + EDGE) * edge_real
            k_imag = amp * (1.0 - EDGE) * edge_imag
            stage_ref[pl.ds(2 * index, FG, stride=TILE_ROWS), :] = k_real * real_part - k_imag * imag_part
            stage_ref[pl.ds(2 * index + 1, FG, stride=TILE_ROWS), :] = k_real * imag_part + k_imag * real_part
            for start, old_real, old_imag in (
                (base, focal_real, focal_imag),
                (tail, edge_real, edge_imag),
            ):
                step_real = turn_ref[0, pl.ds(start, FG), :]
                step_imag = turn_ref[1, pl.ds(start, FG), :]
                phase_ref[0, pl.ds(start, FG), :] = old_real * step_real - old_imag * step_imag
                phase_ref[1, pl.ds(start, FG), :] = old_real * step_imag + old_imag * step_real
            return carry

        lax.fori_loop(0, HALF, one_freq, 0)

    pass_copies = [
        pltpu.make_async_remote_copy(
            src_ref=give_ref.at[parity],
            dst_ref=take_ref.at[parity],
            send_sem=give_sem.at[parity],
            recv_sem=take_sem.at[parity],
            device_id={"elem": sibling},
            device_id_type=MESH,
        )
        for parity in range(2)
    ]
    order = sorted(range(1, freq_count), key=lambda step: -min(step, freq_count - step))
    sends = []
    for parity in range(2):
        freq_scale = (me * W_DEV + parity).astype(jnp.float32) * scale
        start_real, start_imag = unit_phasor(theta_ref[...] * freq_scale)
        phase_ref[0] = start_real
        phase_ref[1] = start_imag
        loads[parity].wait()
        group_spectra(parity, sibling)
        give_ref[parity] = stage_ref[...].astype(jnp.bfloat16)
        if parity == 0:
            pl.semaphore_wait(barrier, freq_count)
        pass_copies[parity].start()
        group_spectra(parity, mine)
        own_ref[...] = stage_ref[...].astype(jnp.bfloat16)
        pass_copies[parity].wait_recv()
        total = own_ref[...].astype(jnp.float32) + take_ref[parity].astype(jnp.float32)
        spec_ref[parity] = total.astype(jnp.bfloat16)
        for step in order:
            peer = lax.rem(me + step, freq_count)
            copy = pltpu.make_async_remote_copy(
                src_ref=spec_ref.at[parity, pl.ds(pl.multiple_of(peer * chunk, chunk), chunk)],
                dst_ref=recv_ref.at[parity, me],
                send_sem=send_sem.at[parity, step],
                recv_sem=recv_sem.at[parity, me],
                device_id={"freq": peer},
                device_id_type=MESH,
            )
            copy.start()
            sends.append(copy)
        recv_ref[parity, me] = spec_ref[parity, pl.ds(pl.multiple_of(me * chunk, chunk), chunk), :]

    def await_half(parity):
        for step in order:
            source = lax.rem(me + step, freq_count)
            pltpu.make_async_remote_copy(
                src_ref=spec_ref.at[parity, pl.ds(0, chunk)],
                dst_ref=recv_ref.at[parity, source],
                send_sem=send_sem.at[parity, step],
                recv_sem=recv_sem.at[parity, source],
                device_id={"freq": source},
                device_id_type=MESH,
            ).wait_recv()

    def half_signal(parity, pair):
        sides = [
            recv_ref[parity, :, pl.ds(pl.multiple_of((2 * pair + side) * TILE_ROWS, TILE_ROWS), TILE_ROWS), :].reshape(
                freq_total, FG
            )
            for side in range(2)
        ]
        both = jnp.concatenate(sides, axis=1)
        return jnp.dot(
            twiddle_ref[parity], jnp.concatenate([both, both], axis=0), preferred_element_type=jnp.float32
        )

    await_half(0)

    def even_pair(pair, carry):
        even_ref[pair] = half_signal(0, pair)
        return carry

    lax.fori_loop(0, columns // 2, even_pair, 0)
    top_ref[...] = jnp.zeros_like(top_ref)
    await_half(1)

    def odd_pair(pair, carry):
        odd = half_signal(1, pair)
        even = even_ref[pair]
        first = even + odd
        second = even - odd
        power = jnp.maximum(
            first[:freq_total] * first[:freq_total] + first[freq_total:] * first[freq_total:],
            second[:freq_total] * second[:freq_total] + second[freq_total:] * second[freq_total:],
        )
        best = jnp.max(power, axis=0, keepdims=True)
        top_ref[pl.ds(2 * pair, 1), :] = best[:, :FG]
        top_ref[pl.ds(2 * pair + 1, 1), :] = best[:, FG:]
        return carry

    lax.fori_loop(0, columns // 2, odd_pair, 0)
    strongest = jnp.max(jnp.transpose(top_ref[...]), axis=0, keepdims=True)[:, :columns]
    flaw_peak = jnp.sqrt(strongest) * (1.0 / math.sqrt(freq_total))
    peak_ref[...] = flaw_peak
    level = STEEP * (jnp.log(flaw_peak + EPS) - jnp.log(noise_ref[...]))
    detection_ref[...] = 1.0 / (1.0 + jnp.exp(-level))
    for copy in pass_copies:
        copy.wait_send()
    for copy in sends:
        copy.wait_send()


def fused_body(
    flaw_cells,
    flaw_blocks,
    element_channel,
    focal_delay,
    beam_field,
    flaw_size,
    flaw_slope,
    noise_level,
):
    freq_count = lax.axis_size("freq")
    columns = FG // freq_count
    elements, cells = beam_field.shape[2:]
    vmem = pl.BlockSpec(memory_space=pltpu.VMEM)
    rows = FG * TILE_ROWS
    chunk = columns * TILE_ROWS
    freq_total = W_DEV * freq_count
    out = jax.ShapeDtypeStruct((1, columns), jnp.float32)
    return pl.pallas_call(
        functools.partial(inspect_kernel, freq_count),
        out_shape=(out, out),
        in_specs=[pl.BlockSpec(memory_space=pltpu.SMEM), vmem, vmem, vmem, pl.BlockSpec(memory_space=pl.ANY)]
        + [vmem] * 4,
        out_specs=(vmem, vmem),
        scratch_shapes=[
            pltpu.VMEM((2, HALF, 2 * elements, cells), jnp.bfloat16),
            pltpu.VMEM((cells, cells), jnp.bfloat16),
            pltpu.VMEM((4 * FG, elements), jnp.float32),
            pltpu.VMEM((2 * FG, elements), jnp.float32),
            pltpu.VMEM((2, 4 * FG, elements), jnp.float32),
            pltpu.VMEM((2, 4 * FG, elements), jnp.float32),
            pltpu.VMEM((rows, FG), jnp.float32),
            pltpu.VMEM((rows, FG), jnp.bfloat16),
            pltpu.VMEM((2, rows, FG), jnp.bfloat16),
            pltpu.VMEM((2, rows, FG), jnp.bfloat16),
            pltpu.VMEM((2, rows, FG), jnp.bfloat16),
            pltpu.VMEM((2, freq_count, chunk, FG), jnp.bfloat16),
            pltpu.VMEM((columns // 2, 2 * freq_total, 2 * FG), jnp.float32),
            pltpu.VMEM((FG, FG), jnp.float32),
            pltpu.SemaphoreType.DMA((2,)),
            pltpu.SemaphoreType.DMA((2,)),
            pltpu.SemaphoreType.DMA((2,)),
            pltpu.SemaphoreType.DMA((2, freq_count)),
            pltpu.SemaphoreType.DMA((2, freq_count)),
        ],
        compiler_params=pltpu.CompilerParams(
            collective_id=0, has_side_effects=True, vmem_limit_bytes=48 << 20
        ),
    )(
        flaw_blocks,
        flaw_cells.reshape(1, cells),
        element_channel.reshape(1, elements),
        focal_delay,
        beam_field.reshape(HALF, 2, 2 * elements, cells),
        flaw_size,
        flaw_slope,
        noise_level,
        jnp.asarray(half_twiddles(freq_count)),
    )


def plain_body(
    flaw_cells,
    flaw_blocks,
    element_channel,
    focal_delay,
    beam_field,
    flaw_size,
    flaw_slope,
    noise_level,
):
    freq_count = lax.axis_size("freq")
    freq_total = W_DEV * freq_count
    group_total = flaw_size.shape[0]
    row_total = NB * SB
    first_freq = lax.axis_index("freq") * W_DEV
    angular = (first_freq + jnp.arange(W_DEV, dtype=jnp.int32)).astype(jnp.float32) * (
        math.pi / freq_total
    )
    scan_rows = (
        flaw_blocks.reshape(group_total, NB)[:, :, None] * SB
        + jnp.arange(SB, dtype=jnp.int32)[None, None, :]
    ).reshape(group_total, row_total)
    delays = jnp.moveaxis(
        jnp.take(jnp.take(focal_delay, element_channel, axis=0), scan_rows, axis=1), 0, 2
    )
    fields = jnp.take(beam_field, flaw_cells, axis=3).reshape(
        W_DEV, 2, element_channel.shape[0], group_total, FG
    )
    k_real, k_imag = kirchhoff(angular, flaw_size, flaw_slope)
    focal_terms = focal_law(angular, delays)
    field_terms = field_matrix(fields)
    product = jnp.einsum(
        "wgre,wegf->gwrf", focal_terms, field_terms, preferred_element_type=jnp.float32
    )
    partial_value = combine(product, k_real, k_imag).astype(jnp.bfloat16)
    rounded_term = lax.optimization_barrier(partial_value).astype(jnp.float32)
    summed = lax.psum_scatter(
        rounded_term.astype(jnp.bfloat16), "elem", scatter_dimension=0, tiled=True
    )
    partial_peak = regroup_peaks(
        lax.all_to_all(summed, "freq", split_axis=3, concat_axis=1, tiled=True)
    )
    whole_peak = lax.pmax(partial_peak, "freq")
    columns = FG // freq_count
    flaw_peak = lax.dynamic_slice_in_dim(whole_peak, lax.axis_index("freq") * columns, columns, 1)
    detection = jax.nn.sigmoid(STEEP * (jnp.log(flaw_peak + EPS) - jnp.log(noise_level)))
    return (flaw_peak, detection)


def solution(mesh):
    in_specs = (
        P("batch"),
        P("batch"),
        P("elem"),
        P(),
        P("freq", None, "elem", None),
        P("batch", None),
        P("batch", None),
        P(("batch", "elem"), "freq"),
    )
    out_specs = (P(("batch", "elem"), "freq"), P(("batch", "elem"), "freq"))
    freq_count = mesh.shape["freq"]
    freq_total = W_DEV * freq_count
    whole_tiles = FG % (2 * freq_count) == 0 and freq_total % FG == 0
    body = fused_body if whole_tiles and 2 * freq_total <= T_CAP else plain_body
    return jax.shard_map(body, mesh=mesh, in_specs=in_specs, out_specs=out_specs, check_vma=False)
```

```python
import functools
import math

import jax
import jax.numpy as jnp
import numpy as np
from jax import lax
from jax.experimental import pallas as pl
from jax.experimental.pallas import tpu as pltpu
from jax.sharding import PartitionSpec as P

W_DEV = 16
FG = 128
NB = 4
SB = 32
T_CAP = 1024


EDGE = 0.6
STEEP = 3.0
EPS = 1e-05


def kirchhoff(angular, flaw_size, flaw_slope):
    angles = angular[None, :, None] * (2.0 * flaw_size * flaw_slope)[:, None, :]
    real_part = flaw_size[:, None, :] * (1.0 + EDGE) * jnp.cos(angles)
    imag_part = flaw_size[:, None, :] * (EDGE - 1.0) * jnp.sin(angles)
    return (real_part, imag_part)


def focal_law(angular, delays):
    phases = angular[:, None, None, None] * delays[None]
    return jnp.concatenate([jnp.cos(phases), -jnp.sin(phases)], axis=-1).astype(jnp.bfloat16)


def field_matrix(fields):
    real_part = fields[:, 0]
    imag_part = fields[:, 1]
    upper_rows = jnp.concatenate([real_part, imag_part], axis=-1)
    lower_rows = jnp.concatenate([-imag_part, real_part], axis=-1)
    return jnp.concatenate([upper_rows, lower_rows], axis=1)


def combine(product, k_real, k_imag):
    columns = k_real.shape[-1]
    real_part = product[..., :columns]
    imag_part = product[..., columns:]
    scale_real = k_real[:, :, None, :]
    scale_imag = k_imag[:, :, None, :]
    return jnp.stack(
        [
            scale_real * real_part - scale_imag * imag_part,
            scale_real * imag_part + scale_imag * real_part,
        ],
        axis=2,
    )


def envelope_peak(spectra, row_count):
    groups, freq_total, planes, columns = spectra.shape
    sample_count = min(T_CAP, 2 * freq_total)
    time_block = min(128, sample_count)
    freq_index = jnp.arange(freq_total, dtype=jnp.int32)
    scaling = 1.0 / math.sqrt(freq_total)

    def advance(step_index, running):
        sample_times = step_index * time_block + jnp.arange(time_block, dtype=jnp.int32)
        phase_steps = freq_index[:, None] * sample_times[None, :] % (2 * freq_total)
        angles = phase_steps.astype(jnp.float32) * (math.pi / freq_total)
        cosine = jnp.cos(angles)
        sine_part = jnp.sin(angles)
        twiddle = jnp.stack(
            [jnp.stack([cosine, sine_part], axis=1), jnp.stack([-sine_part, cosine], axis=1)],
            axis=1,
        )
        twiddle_high = lax.optimization_barrier(twiddle.astype(jnp.bfloat16))
        twiddle_low = (twiddle - twiddle_high.astype(jnp.float32)).astype(jnp.bfloat16)
        signal = jnp.einsum(
            "gwcx,wckt->gkxt", spectra, twiddle_high, preferred_element_type=jnp.float32
        )
        signal = signal + jnp.einsum(
            "gwcx,wckt->gkxt", spectra, twiddle_low, preferred_element_type=jnp.float32
        )
        signal = signal * scaling
        magnitude = jnp.sqrt(signal[:, 0] * signal[:, 0] + signal[:, 1] * signal[:, 1])
        magnitude = magnitude.reshape(groups, row_count, columns // row_count, time_block)
        return jnp.maximum(running, jnp.max(magnitude, axis=(1, 3)))

    initial = jnp.zeros((groups, columns // row_count), jnp.float32)
    return lax.fori_loop(0, sample_count // time_block, advance, initial)


def regroup_peaks(moved):
    groups, freq_total, planes, row_count, flaw_count = moved.shape
    return envelope_peak(
        moved.reshape(groups, freq_total, planes, row_count * flaw_count), row_count
    )


MESH = pl.DeviceIdType.MESH
HALF = W_DEV // 2
TILE_ROWS = 2 * HALF
NT_DIMS = (((1,), (1,)), ((), ()))


def dot_rows(left, right):
    return lax.dot_general(left, right, NT_DIMS, preferred_element_type=jnp.float32)


def unit_phasor(turns):
    rest = turns - jnp.floor(turns + 0.5)
    angle = rest * math.pi
    square = angle * angle
    sine = jnp.full_like(angle, -1.0 / math.factorial(11))
    for order, sign in ((9, 1.0), (7, -1.0), (5, 1.0), (3, -1.0), (1, 1.0)):
        sine = sine * square + sign / math.factorial(order)
    sine = sine * angle
    cosine = jnp.full_like(angle, 1.0 / math.factorial(12))
    for order, sign in ((10, -1.0), (8, 1.0), (6, -1.0), (4, 1.0), (2, -1.0), (0, 1.0)):
        cosine = cosine * square + sign / math.factorial(order)
    return 1.0 - 2.0 * sine * sine, -2.0 * sine * cosine


def half_twiddles(freq_count):
    freq_total = W_DEV * freq_count
    samples = np.arange(freq_total)
    halves = []
    for parity in range(2):
        freqs = (np.arange(freq_count)[:, None] * W_DEV + 2 * np.arange(HALF)[None, :] + parity).reshape(-1)
        angles = (samples[:, None] * freqs[None, :] % (2 * freq_total)) * (np.pi / freq_total)
        cosine, sine = np.cos(angles), np.sin(angles)
        real_rows = np.stack([cosine, -sine], axis=-1).reshape(freq_total, -1)
        imag_rows = np.stack([sine, cosine], axis=-1).reshape(freq_total, -1)
        whole = np.concatenate([real_rows, imag_rows], axis=0).astype(np.float32)
        high = whole.astype(jnp.bfloat16)
        low = (whole - high.astype(np.float32)).astype(jnp.bfloat16)
        halves.append(np.concatenate([high, low], axis=1))
    return np.stack(halves)


def inspect_kernel(
    freq_count,
    blocks_hbm,
    cells_hbm,
    channel_hbm,
    delay_hbm,
    field_hbm,
    size_hbm,
    slope_hbm,
    twiddle_hbm,
    power_ref,
    blocks_ref,
    cells_ref,
    channel_ref,
    delay_ref,
    size_ref,
    slope_ref,
    twiddle_ref,
    field_ref,
    select_ref,
    theta_ref,
    amp_ref,
    phase_ref,
    turn_ref,
    stage_ref,
    own_ref,
    give_ref,
    take_ref,
    spec_ref,
    recv_ref,
    even_ref,
    top_ref,
    load_sem,
    field_sem,
    give_sem,
    take_sem,
    send_sem,
    recv_sem,
):
    freq_total = W_DEV * freq_count
    columns = FG // freq_count
    chunk = columns * TILE_ROWS
    me = lax.axis_index("freq")
    mine = lax.axis_index("elem")
    sibling = 1 - mine

    small = [
        pltpu.make_async_copy(source, target, load_sem.at[index])
        for index, (source, target) in enumerate(
            (
                (cells_hbm, cells_ref),
                (channel_hbm, channel_ref),
                (blocks_hbm, blocks_ref),
                (delay_hbm, delay_ref),
                (size_hbm, size_ref),
                (slope_hbm, slope_ref),
                (twiddle_hbm, twiddle_ref),
            )
        )
    ]
    for load in small[:-1]:
        load.start()
    loads = [
        pltpu.make_async_copy(field_hbm.at[:, parity], field_ref.at[parity], field_sem.at[parity])
        for parity in range(2)
    ]
    for load in loads:
        load.start()
    small[-1].start()

    barrier = pltpu.get_barrier_semaphore()
    pl.semaphore_signal(barrier, inc=1, device_id={"elem": sibling}, device_id_type=MESH)
    for step in range(1, freq_count):
        pl.semaphore_signal(
            barrier, inc=1, device_id={"freq": lax.rem(me + step, freq_count)}, device_id_type=MESH
        )

    small[0].wait()
    cell_count = cells_ref.shape[1]
    cell_rows = lax.broadcasted_iota(jnp.int32, (cell_count, cell_count), 0)
    chosen = jnp.where(cell_rows == cells_ref[...], 1.0, 0.0)
    select_ref[...] = jnp.transpose(chosen).astype(jnp.bfloat16)

    for load in small[1:-1]:
        load.wait()
    channel_count, scan_count = delay_ref.shape
    element_count = channel_ref.shape[1]
    channel_rows = lax.broadcasted_iota(jnp.int32, (channel_count, element_count), 0)
    drives = jnp.transpose(jnp.where(channel_rows == channel_ref[...], 1.0, 0.0)).astype(jnp.bfloat16)
    sub = lax.broadcasted_iota(jnp.int32, (SB, scan_count), 0)
    lane = lax.broadcasted_iota(jnp.int32, (SB, scan_count), 1)
    rows = jnp.concatenate(
        [jnp.where(lane == sub + blocks_ref[j] * SB, 1.0, 0.0) for j in range(2 * NB)], axis=0
    ).astype(jnp.bfloat16)
    rest = delay_ref[...]
    delays = jnp.zeros((2 * FG, element_count), jnp.float32)
    for _ in range(3):
        piece = rest.astype(jnp.bfloat16)
        rest = rest - piece.astype(jnp.float32)
        by_element = jnp.dot(drives, piece, preferred_element_type=jnp.float32).astype(jnp.bfloat16)
        delays = delays + dot_rows(rows, by_element)
    theta_ref[: 2 * FG] = delays
    for group in range(2):
        size = jnp.transpose(jnp.broadcast_to(size_ref[group : group + 1, :], (FG, FG)))
        slope = jnp.transpose(jnp.broadcast_to(slope_ref[group : group + 1, :], (FG, FG)))
        theta_ref[(2 + group) * FG : (3 + group) * FG] = 2.0 * size * slope
        amp_ref[group * FG : (group + 1) * FG] = size
    scale = 0.5 / freq_total
    turn_real, turn_imag = unit_phasor(theta_ref[...] * (2.0 * scale))
    turn_ref[0] = turn_real
    turn_ref[1] = turn_imag

    def group_spectra(parity, group):
        base = pl.multiple_of(group * FG, FG)
        tail = pl.multiple_of((2 + group) * FG, FG)

        def one_freq(index, carry):
            focal_real = phase_ref[0, pl.ds(base, FG), :]
            focal_imag = phase_ref[1, pl.ds(base, FG), :]
            fields = dot_rows(select_ref[pl.ds(base, FG), :], field_ref[parity, index])
            weights = jnp.concatenate(
                [
                    jnp.concatenate([focal_real, -focal_imag], axis=1),
                    jnp.concatenate([focal_imag, focal_real], axis=1),
                ],
                axis=0,
            ).astype(jnp.bfloat16)
            product = dot_rows(fields.astype(jnp.bfloat16), weights)
            real_part = product[:, :FG]
            imag_part = product[:, FG:]
            edge_real = phase_ref[0, pl.ds(tail, FG), :]
            edge_imag = phase_ref[1, pl.ds(tail, FG), :]
            amp = amp_ref[pl.ds(base, FG), :]
            k_real = amp * (1.0 + EDGE) * edge_real
            k_imag = amp * (1.0 - EDGE) * edge_imag
            stage_ref[pl.ds(2 * index, FG, stride=TILE_ROWS), :] = k_real * real_part - k_imag * imag_part
            stage_ref[pl.ds(2 * index + 1, FG, stride=TILE_ROWS), :] = k_real * imag_part + k_imag * real_part
            for start, old_real, old_imag in (
                (base, focal_real, focal_imag),
                (tail, edge_real, edge_imag),
            ):
                step_real = turn_ref[0, pl.ds(start, FG), :]
                step_imag = turn_ref[1, pl.ds(start, FG), :]
                phase_ref[0, pl.ds(start, FG), :] = old_real * step_real - old_imag * step_imag
                phase_ref[1, pl.ds(start, FG), :] = old_real * step_imag + old_imag * step_real
            return carry

        lax.fori_loop(0, HALF, one_freq, 0)

    pass_copies = [
        pltpu.make_async_remote_copy(
            src_ref=give_ref.at[parity],
            dst_ref=take_ref.at[parity],
            send_sem=give_sem.at[parity],
            recv_sem=take_sem.at[parity],
            device_id={"elem": sibling},
            device_id_type=MESH,
        )
        for parity in range(2)
    ]
    half_count = freq_count // 2
    side = me // half_count
    peers = [(1 - side) * half_count + lax.rem(me + step, half_count) for step in range(half_count)]
    peers += [side * half_count + lax.rem(me + step, half_count) for step in range(1, half_count)]
    sends = []
    for parity in range(2):
        freq_scale = (me * W_DEV + parity).astype(jnp.float32) * scale
        start_real, start_imag = unit_phasor(theta_ref[...] * freq_scale)
        phase_ref[0] = start_real
        phase_ref[1] = start_imag
        loads[parity].wait()
        group_spectra(parity, sibling)
        give_ref[parity] = stage_ref[...].astype(jnp.bfloat16)
        if parity == 0:
            pl.semaphore_wait(barrier, freq_count)
        pass_copies[parity].start()
        group_spectra(parity, mine)
        own_ref[...] = stage_ref[...].astype(jnp.bfloat16)
        pass_copies[parity].wait_recv()
        total = own_ref[...].astype(jnp.float32) + take_ref[parity].astype(jnp.float32)
        spec_ref[parity] = total.astype(jnp.bfloat16)
        for step, peer in enumerate(peers):
            copy = pltpu.make_async_remote_copy(
                src_ref=spec_ref.at[parity, pl.ds(pl.multiple_of(peer * chunk, chunk), chunk)],
                dst_ref=recv_ref.at[parity, me],
                send_sem=send_sem.at[parity, step],
                recv_sem=recv_sem.at[parity, me],
                device_id={"freq": peer},
                device_id_type=MESH,
            )
            copy.start()
            sends.append(copy)
        recv_ref[parity, me] = spec_ref[parity, pl.ds(pl.multiple_of(me * chunk, chunk), chunk), :]

    def await_half(parity):
        for step, source in enumerate(peers):
            pltpu.make_async_remote_copy(
                src_ref=spec_ref.at[parity, pl.ds(0, chunk)],
                dst_ref=recv_ref.at[parity, source],
                send_sem=send_sem.at[parity, step],
                recv_sem=recv_sem.at[parity, source],
                device_id={"freq": source},
                device_id_type=MESH,
            ).wait_recv()

    def half_signal(parity, pair):
        sides = [
            recv_ref[parity, :, pl.ds(pl.multiple_of((2 * pair + side) * TILE_ROWS, TILE_ROWS), TILE_ROWS), :].reshape(
                freq_total, FG
            )
            for side in range(2)
        ]
        both = jnp.concatenate(sides, axis=1)
        return jnp.dot(
            twiddle_ref[parity], jnp.concatenate([both, both], axis=0), preferred_element_type=jnp.float32
        )

    small[-1].wait()
    await_half(0)

    def even_pair(pair, carry):
        even_ref[pair] = half_signal(0, pair)
        return carry

    lax.fori_loop(0, columns // 2, even_pair, 0)
    top_ref[...] = jnp.zeros_like(top_ref)
    await_half(1)

    def odd_pair(pair, carry):
        odd = half_signal(1, pair)
        even = even_ref[pair]
        first = even + odd
        second = even - odd
        power = jnp.maximum(
            first[:freq_total] * first[:freq_total] + first[freq_total:] * first[freq_total:],
            second[:freq_total] * second[:freq_total] + second[freq_total:] * second[freq_total:],
        )
        best = jnp.max(power, axis=0, keepdims=True)
        top_ref[pl.ds(2 * pair, 1), :] = best[:, :FG]
        top_ref[pl.ds(2 * pair + 1, 1), :] = best[:, FG:]
        return carry

    lax.fori_loop(0, columns // 2, odd_pair, 0)
    power_ref[...] = jnp.max(jnp.transpose(top_ref[...]), axis=0, keepdims=True)
    for copy in pass_copies:
        copy.wait_send()
    for copy in sends:
        copy.wait_send()


def fused_body(
    flaw_cells,
    flaw_blocks,
    element_channel,
    focal_delay,
    beam_field,
    flaw_size,
    flaw_slope,
    noise_level,
):
    freq_count = lax.axis_size("freq")
    columns = FG // freq_count
    elements, cells = beam_field.shape[2:]
    vmem = pl.BlockSpec(memory_space=pltpu.VMEM)
    rows = FG * TILE_ROWS
    chunk = columns * TILE_ROWS
    freq_total = W_DEV * freq_count
    hbm = pl.BlockSpec(memory_space=pltpu.MemorySpace.HBM)
    power = pl.pallas_call(
        functools.partial(inspect_kernel, freq_count),
        out_shape=jax.ShapeDtypeStruct((1, FG), jnp.float32),
        in_specs=[hbm] * 8,
        out_specs=vmem,
        scratch_shapes=[
            pltpu.SMEM(flaw_blocks.shape, jnp.int32),
            pltpu.VMEM((1, cells), jnp.int32),
            pltpu.VMEM((1, elements), jnp.int32),
            pltpu.VMEM(focal_delay.shape, jnp.float32),
            pltpu.VMEM(flaw_size.shape, jnp.float32),
            pltpu.VMEM(flaw_slope.shape, jnp.float32),
            pltpu.VMEM((2, 2 * freq_total, 2 * freq_total), jnp.bfloat16),
            pltpu.VMEM((2, HALF, 2 * elements, cells), jnp.bfloat16),
            pltpu.VMEM((cells, cells), jnp.bfloat16),
            pltpu.VMEM((4 * FG, elements), jnp.float32),
            pltpu.VMEM((2 * FG, elements), jnp.float32),
            pltpu.VMEM((2, 4 * FG, elements), jnp.float32),
            pltpu.VMEM((2, 4 * FG, elements), jnp.float32),
            pltpu.VMEM((rows, FG), jnp.float32),
            pltpu.VMEM((rows, FG), jnp.bfloat16),
            pltpu.VMEM((2, rows, FG), jnp.bfloat16),
            pltpu.VMEM((2, rows, FG), jnp.bfloat16),
            pltpu.VMEM((2, rows, FG), jnp.bfloat16),
            pltpu.VMEM((2, freq_count, chunk, FG), jnp.bfloat16),
            pltpu.VMEM((columns // 2, 2 * freq_total, 2 * FG), jnp.float32),
            pltpu.VMEM((FG, FG), jnp.float32),
            pltpu.SemaphoreType.DMA((7,)),
            pltpu.SemaphoreType.DMA((2,)),
            pltpu.SemaphoreType.DMA((2,)),
            pltpu.SemaphoreType.DMA((2,)),
            pltpu.SemaphoreType.DMA((2, freq_count)),
            pltpu.SemaphoreType.DMA((2, freq_count)),
        ],
        compiler_params=pltpu.CompilerParams(
            collective_id=0, has_side_effects=True, vmem_limit_bytes=67_043_328
        ),
    )(
        flaw_blocks,
        flaw_cells.reshape(1, cells),
        element_channel.reshape(1, elements),
        focal_delay,
        beam_field.reshape(HALF, 2, 2 * elements, cells),
        flaw_size,
        flaw_slope,
        jnp.asarray(half_twiddles(freq_count)),
    )
    flaw_peak = jnp.sqrt(power[:, :columns]) * (1.0 / math.sqrt(freq_total))
    detection = jax.nn.sigmoid(STEEP * (jnp.log(flaw_peak + EPS) - jnp.log(noise_level)))
    return (flaw_peak, detection)


def plain_body(
    flaw_cells,
    flaw_blocks,
    element_channel,
    focal_delay,
    beam_field,
    flaw_size,
    flaw_slope,
    noise_level,
):
    freq_count = lax.axis_size("freq")
    freq_total = W_DEV * freq_count
    group_total = flaw_size.shape[0]
    row_total = NB * SB
    first_freq = lax.axis_index("freq") * W_DEV
    angular = (first_freq + jnp.arange(W_DEV, dtype=jnp.int32)).astype(jnp.float32) * (
        math.pi / freq_total
    )
    scan_rows = (
        flaw_blocks.reshape(group_total, NB)[:, :, None] * SB
        + jnp.arange(SB, dtype=jnp.int32)[None, None, :]
    ).reshape(group_total, row_total)
    delays = jnp.moveaxis(
        jnp.take(jnp.take(focal_delay, element_channel, axis=0), scan_rows, axis=1), 0, 2
    )
    fields = jnp.take(beam_field, flaw_cells, axis=3).reshape(
        W_DEV, 2, element_channel.shape[0], group_total, FG
    )
    k_real, k_imag = kirchhoff(angular, flaw_size, flaw_slope)
    focal_terms = focal_law(angular, delays)
    field_terms = field_matrix(fields)
    product = jnp.einsum(
        "wgre,wegf->gwrf", focal_terms, field_terms, preferred_element_type=jnp.float32
    )
    partial_value = combine(product, k_real, k_imag).astype(jnp.bfloat16)
    rounded_term = lax.optimization_barrier(partial_value).astype(jnp.float32)
    summed = lax.psum_scatter(
        rounded_term.astype(jnp.bfloat16), "elem", scatter_dimension=0, tiled=True
    )
    partial_peak = regroup_peaks(
        lax.all_to_all(summed, "freq", split_axis=3, concat_axis=1, tiled=True)
    )
    whole_peak = lax.pmax(partial_peak, "freq")
    columns = FG // freq_count
    flaw_peak = lax.dynamic_slice_in_dim(whole_peak, lax.axis_index("freq") * columns, columns, 1)
    detection = jax.nn.sigmoid(STEEP * (jnp.log(flaw_peak + EPS) - jnp.log(noise_level)))
    return (flaw_peak, detection)


def solution(mesh):
    in_specs = (
        P("batch"),
        P("batch"),
        P("elem"),
        P(),
        P("freq", None, "elem", None),
        P("batch", None),
        P("batch", None),
        P(("batch", "elem"), "freq"),
    )
    out_specs = (P(("batch", "elem"), "freq"), P(("batch", "elem"), "freq"))
    freq_count = mesh.shape["freq"]
    freq_total = W_DEV * freq_count
    whole_tiles = FG % (2 * freq_count) == 0 and freq_total % FG == 0
    body = fused_body if whole_tiles and 2 * freq_total <= T_CAP else plain_body
    return jax.shard_map(body, mesh=mesh, in_specs=in_specs, out_specs=out_specs, check_vma=False)
```

```python
import functools
import math

import jax
import jax.numpy as jnp
import numpy as np
from jax import lax
from jax.experimental import pallas as pl
from jax.experimental.pallas import tpu as pltpu
from jax.sharding import PartitionSpec as P

W_DEV = 16
FG = 128
NB = 4
SB = 32
T_CAP = 1024


EDGE = 0.6
STEEP = 3.0
EPS = 1e-05


def kirchhoff(angular, flaw_size, flaw_slope):
    angles = angular[None, :, None] * (2.0 * flaw_size * flaw_slope)[:, None, :]
    real_part = flaw_size[:, None, :] * (1.0 + EDGE) * jnp.cos(angles)
    imag_part = flaw_size[:, None, :] * (EDGE - 1.0) * jnp.sin(angles)
    return (real_part, imag_part)


def focal_law(angular, delays):
    phases = angular[:, None, None, None] * delays[None]
    return jnp.concatenate([jnp.cos(phases), -jnp.sin(phases)], axis=-1).astype(jnp.bfloat16)


def field_matrix(fields):
    real_part = fields[:, 0]
    imag_part = fields[:, 1]
    upper_rows = jnp.concatenate([real_part, imag_part], axis=-1)
    lower_rows = jnp.concatenate([-imag_part, real_part], axis=-1)
    return jnp.concatenate([upper_rows, lower_rows], axis=1)


def combine(product, k_real, k_imag):
    columns = k_real.shape[-1]
    real_part = product[..., :columns]
    imag_part = product[..., columns:]
    scale_real = k_real[:, :, None, :]
    scale_imag = k_imag[:, :, None, :]
    return jnp.stack(
        [
            scale_real * real_part - scale_imag * imag_part,
            scale_real * imag_part + scale_imag * real_part,
        ],
        axis=2,
    )


def envelope_peak(spectra, row_count):
    groups, freq_total, planes, columns = spectra.shape
    sample_count = min(T_CAP, 2 * freq_total)
    time_block = min(128, sample_count)
    freq_index = jnp.arange(freq_total, dtype=jnp.int32)
    scaling = 1.0 / math.sqrt(freq_total)

    def advance(step_index, running):
        sample_times = step_index * time_block + jnp.arange(time_block, dtype=jnp.int32)
        phase_steps = freq_index[:, None] * sample_times[None, :] % (2 * freq_total)
        angles = phase_steps.astype(jnp.float32) * (math.pi / freq_total)
        cosine = jnp.cos(angles)
        sine_part = jnp.sin(angles)
        twiddle = jnp.stack(
            [jnp.stack([cosine, sine_part], axis=1), jnp.stack([-sine_part, cosine], axis=1)],
            axis=1,
        )
        twiddle_high = lax.optimization_barrier(twiddle.astype(jnp.bfloat16))
        twiddle_low = (twiddle - twiddle_high.astype(jnp.float32)).astype(jnp.bfloat16)
        signal = jnp.einsum(
            "gwcx,wckt->gkxt", spectra, twiddle_high, preferred_element_type=jnp.float32
        )
        signal = signal + jnp.einsum(
            "gwcx,wckt->gkxt", spectra, twiddle_low, preferred_element_type=jnp.float32
        )
        signal = signal * scaling
        magnitude = jnp.sqrt(signal[:, 0] * signal[:, 0] + signal[:, 1] * signal[:, 1])
        magnitude = magnitude.reshape(groups, row_count, columns // row_count, time_block)
        return jnp.maximum(running, jnp.max(magnitude, axis=(1, 3)))

    initial = jnp.zeros((groups, columns // row_count), jnp.float32)
    return lax.fori_loop(0, sample_count // time_block, advance, initial)


def regroup_peaks(moved):
    groups, freq_total, planes, row_count, flaw_count = moved.shape
    return envelope_peak(
        moved.reshape(groups, freq_total, planes, row_count * flaw_count), row_count
    )


MESH = pl.DeviceIdType.MESH
HALF = W_DEV // 2
TILE_ROWS = 2 * HALF
NT_DIMS = (((1,), (1,)), ((), ()))


def dot_rows(left, right):
    return lax.dot_general(left, right, NT_DIMS, preferred_element_type=jnp.float32)


def unit_phasor(turns):
    rest = turns - jnp.floor(turns + 0.5)
    angle = rest * math.pi
    square = angle * angle
    sine = jnp.full_like(angle, -1.0 / math.factorial(11))
    for order, sign in ((9, 1.0), (7, -1.0), (5, 1.0), (3, -1.0), (1, 1.0)):
        sine = sine * square + sign / math.factorial(order)
    sine = sine * angle
    cosine = jnp.full_like(angle, 1.0 / math.factorial(12))
    for order, sign in ((10, -1.0), (8, 1.0), (6, -1.0), (4, 1.0), (2, -1.0), (0, 1.0)):
        cosine = cosine * square + sign / math.factorial(order)
    return 1.0 - 2.0 * sine * sine, -2.0 * sine * cosine


def half_twiddles(freq_count):
    freq_total = W_DEV * freq_count
    samples = np.arange(freq_total)
    halves = []
    for parity in range(2):
        freqs = (np.arange(freq_count)[:, None] * W_DEV + 2 * np.arange(HALF)[None, :] + parity).reshape(-1)
        angles = (samples[:, None] * freqs[None, :] % (2 * freq_total)) * (np.pi / freq_total)
        cosine, sine = np.cos(angles), np.sin(angles)
        real_rows = np.stack([cosine, -sine], axis=-1).reshape(freq_total, -1)
        imag_rows = np.stack([sine, cosine], axis=-1).reshape(freq_total, -1)
        whole = np.concatenate([real_rows, imag_rows], axis=0).astype(np.float32)
        high = whole.astype(jnp.bfloat16)
        low = (whole - high.astype(np.float32)).astype(jnp.bfloat16)
        halves.append(np.concatenate([high, low], axis=1))
    return np.stack(halves)


def inspect_kernel(
    freq_count,
    blocks_hbm,
    cells_hbm,
    channel_hbm,
    delay_hbm,
    field_hbm,
    size_hbm,
    slope_hbm,
    twiddle_hbm,
    power_ref,
    blocks_ref,
    cells_ref,
    channel_ref,
    delay_ref,
    size_ref,
    slope_ref,
    twiddle_ref,
    field_ref,
    select_ref,
    theta_ref,
    amp_ref,
    phase_ref,
    turn_ref,
    stage_ref,
    own_ref,
    give_ref,
    take_ref,
    spec_ref,
    recv_ref,
    even_ref,
    top_ref,
    load_sem,
    field_sem,
    give_sem,
    take_sem,
    send_sem,
    recv_sem,
):
    freq_total = W_DEV * freq_count
    columns = FG // freq_count
    chunk = columns * TILE_ROWS
    me = lax.axis_index("freq")
    mine = lax.axis_index("elem")
    sibling = 1 - mine

    small = [
        pltpu.make_async_copy(source, target, load_sem.at[index])
        for index, (source, target) in enumerate(
            (
                (cells_hbm, cells_ref),
                (channel_hbm, channel_ref),
                (blocks_hbm, blocks_ref),
                (delay_hbm, delay_ref),
                (size_hbm, size_ref),
                (slope_hbm, slope_ref),
                (twiddle_hbm, twiddle_ref),
            )
        )
    ]
    for load in small[:-1]:
        load.start()
    loads = [
        pltpu.make_async_copy(field_hbm.at[:, parity], field_ref.at[parity], field_sem.at[parity])
        for parity in range(2)
    ]
    for load in loads:
        load.start()
    small[-1].start()

    barrier = pltpu.get_barrier_semaphore()
    pl.semaphore_signal(barrier, inc=1, device_id={"elem": sibling}, device_id_type=MESH)
    for step in range(1, freq_count):
        pl.semaphore_signal(
            barrier, inc=1, device_id={"freq": lax.rem(me + step, freq_count)}, device_id_type=MESH
        )

    small[0].wait()
    cell_count = cells_ref.shape[1]
    cell_rows = lax.broadcasted_iota(jnp.int32, (cell_count, cell_count), 0)
    chosen = jnp.where(cell_rows == cells_ref[...], 1.0, 0.0)
    select_ref[...] = jnp.transpose(chosen).astype(jnp.bfloat16)

    for load in small[1:-1]:
        load.wait()
    channel_count, scan_count = delay_ref.shape
    element_count = channel_ref.shape[1]
    channel_rows = lax.broadcasted_iota(jnp.int32, (channel_count, element_count), 0)
    drives = jnp.transpose(jnp.where(channel_rows == channel_ref[...], 1.0, 0.0)).astype(jnp.bfloat16)
    sub = lax.broadcasted_iota(jnp.int32, (SB, scan_count), 0)
    lane = lax.broadcasted_iota(jnp.int32, (SB, scan_count), 1)
    rows = jnp.concatenate(
        [jnp.where(lane == sub + blocks_ref[j] * SB, 1.0, 0.0) for j in range(2 * NB)], axis=0
    ).astype(jnp.bfloat16)
    rest = delay_ref[...]
    delays = jnp.zeros((2 * FG, element_count), jnp.float32)
    for _ in range(3):
        piece = rest.astype(jnp.bfloat16)
        rest = rest - piece.astype(jnp.float32)
        by_element = jnp.dot(drives, piece, preferred_element_type=jnp.float32).astype(jnp.bfloat16)
        delays = delays + dot_rows(rows, by_element)
    theta_ref[: 2 * FG] = delays
    for group in range(2):
        size = jnp.transpose(jnp.broadcast_to(size_ref[group : group + 1, :], (FG, FG)))
        slope = jnp.transpose(jnp.broadcast_to(slope_ref[group : group + 1, :], (FG, FG)))
        theta_ref[(2 + group) * FG : (3 + group) * FG] = 2.0 * size * slope
        amp_ref[group * FG : (group + 1) * FG] = size
    scale = 0.5 / freq_total
    turn_real, turn_imag = unit_phasor(theta_ref[...] * (2.0 * scale))
    turn_ref[0] = turn_real
    turn_ref[1] = turn_imag

    def group_spectra(parity, group):
        base = pl.multiple_of(group * FG, FG)
        tail = pl.multiple_of((2 + group) * FG, FG)

        def one_freq(index, carry):
            focal_real = phase_ref[0, pl.ds(base, FG), :]
            focal_imag = phase_ref[1, pl.ds(base, FG), :]
            fields = dot_rows(select_ref[pl.ds(base, FG), :], field_ref[parity, index])
            weights = jnp.concatenate(
                [
                    jnp.concatenate([focal_real, -focal_imag], axis=1),
                    jnp.concatenate([focal_imag, focal_real], axis=1),
                ],
                axis=0,
            ).astype(jnp.bfloat16)
            product = dot_rows(fields.astype(jnp.bfloat16), weights)
            real_part = product[:, :FG]
            imag_part = product[:, FG:]
            edge_real = phase_ref[0, pl.ds(tail, FG), :]
            edge_imag = phase_ref[1, pl.ds(tail, FG), :]
            amp = amp_ref[pl.ds(base, FG), :]
            k_real = amp * (1.0 + EDGE) * edge_real
            k_imag = amp * (1.0 - EDGE) * edge_imag
            stage_ref[pl.ds(2 * index, FG, stride=TILE_ROWS), :] = k_real * real_part - k_imag * imag_part
            stage_ref[pl.ds(2 * index + 1, FG, stride=TILE_ROWS), :] = k_real * imag_part + k_imag * real_part
            for start, old_real, old_imag in (
                (base, focal_real, focal_imag),
                (tail, edge_real, edge_imag),
            ):
                step_real = turn_ref[0, pl.ds(start, FG), :]
                step_imag = turn_ref[1, pl.ds(start, FG), :]
                phase_ref[0, pl.ds(start, FG), :] = old_real * step_real - old_imag * step_imag
                phase_ref[1, pl.ds(start, FG), :] = old_real * step_imag + old_imag * step_real
            return carry

        lax.fori_loop(0, HALF, one_freq, 0, unroll=2)

    pass_copies = [
        pltpu.make_async_remote_copy(
            src_ref=give_ref.at[parity],
            dst_ref=take_ref.at[parity],
            send_sem=give_sem.at[parity],
            recv_sem=take_sem.at[parity],
            device_id={"elem": sibling},
            device_id_type=MESH,
        )
        for parity in range(2)
    ]
    half_count = freq_count // 2
    side = me // half_count
    peers = [(1 - side) * half_count + lax.rem(me + step, half_count) for step in range(half_count)]
    peers += [side * half_count + lax.rem(me + step, half_count) for step in range(1, half_count)]
    sends = []
    for parity in range(2):
        freq_scale = (me * W_DEV + parity).astype(jnp.float32) * scale
        start_real, start_imag = unit_phasor(theta_ref[...] * freq_scale)
        phase_ref[0] = start_real
        phase_ref[1] = start_imag
        loads[parity].wait()
        group_spectra(parity, sibling)
        give_ref[parity] = stage_ref[...].astype(jnp.bfloat16)
        if parity == 0:
            pl.semaphore_wait(barrier, freq_count)
        pass_copies[parity].start()
        group_spectra(parity, mine)
        own_ref[...] = stage_ref[...].astype(jnp.bfloat16)
        pass_copies[parity].wait_recv()
        total = own_ref[...].astype(jnp.float32) + take_ref[parity].astype(jnp.float32)
        spec_ref[parity] = total.astype(jnp.bfloat16)
        for step, peer in enumerate(peers):
            copy = pltpu.make_async_remote_copy(
                src_ref=spec_ref.at[parity, pl.ds(pl.multiple_of(peer * chunk, chunk), chunk)],
                dst_ref=recv_ref.at[parity, me],
                send_sem=send_sem.at[parity, step],
                recv_sem=recv_sem.at[parity, me],
                device_id={"freq": peer},
                device_id_type=MESH,
            )
            copy.start()
            sends.append(copy)
        recv_ref[parity, me] = spec_ref[parity, pl.ds(pl.multiple_of(me * chunk, chunk), chunk), :]

    def await_half(parity):
        for step, source in enumerate(peers):
            pltpu.make_async_remote_copy(
                src_ref=spec_ref.at[parity, pl.ds(0, chunk)],
                dst_ref=recv_ref.at[parity, source],
                send_sem=send_sem.at[parity, step],
                recv_sem=recv_sem.at[parity, source],
                device_id={"freq": source},
                device_id_type=MESH,
            ).wait_recv()

    def half_signal(parity, pair):
        sides = [
            recv_ref[parity, :, pl.ds(pl.multiple_of((2 * pair + side) * TILE_ROWS, TILE_ROWS), TILE_ROWS), :].reshape(
                freq_total, FG
            )
            for side in range(2)
        ]
        both = jnp.concatenate(sides, axis=1)
        return jnp.dot(
            twiddle_ref[parity], jnp.concatenate([both, both], axis=0), preferred_element_type=jnp.float32
        )

    small[-1].wait()
    await_half(0)

    def even_pair(pair, carry):
        even_ref[pair] = half_signal(0, pair)
        return carry

    lax.fori_loop(0, columns // 2, even_pair, 0)
    top_ref[...] = jnp.zeros_like(top_ref)
    await_half(1)

    def odd_pair(pair, carry):
        odd = half_signal(1, pair)
        even = even_ref[pair]
        first = even + odd
        second = even - odd
        power = jnp.maximum(
            first[:freq_total] * first[:freq_total] + first[freq_total:] * first[freq_total:],
            second[:freq_total] * second[:freq_total] + second[freq_total:] * second[freq_total:],
        )
        best = jnp.max(power, axis=0, keepdims=True)
        top_ref[pl.ds(2 * pair, 1), :] = best[:, :FG]
        top_ref[pl.ds(2 * pair + 1, 1), :] = best[:, FG:]
        return carry

    lax.fori_loop(0, columns // 2, odd_pair, 0, unroll=4 if columns % 8 == 0 else 1)
    power_ref[...] = jnp.max(jnp.transpose(top_ref[...]), axis=0, keepdims=True)
    for copy in pass_copies:
        copy.wait_send()
    for copy in sends:
        copy.wait_send()


def fused_body(
    flaw_cells,
    flaw_blocks,
    element_channel,
    focal_delay,
    beam_field,
    flaw_size,
    flaw_slope,
    noise_level,
):
    freq_count = lax.axis_size("freq")
    columns = FG // freq_count
    elements, cells = beam_field.shape[2:]
    vmem = pl.BlockSpec(memory_space=pltpu.VMEM)
    rows = FG * TILE_ROWS
    chunk = columns * TILE_ROWS
    freq_total = W_DEV * freq_count
    hbm = pl.BlockSpec(memory_space=pltpu.MemorySpace.HBM)
    power = pl.pallas_call(
        functools.partial(inspect_kernel, freq_count),
        out_shape=jax.ShapeDtypeStruct((1, FG), jnp.float32),
        in_specs=[hbm] * 8,
        out_specs=vmem,
        scratch_shapes=[
            pltpu.SMEM(flaw_blocks.shape, jnp.int32),
            pltpu.VMEM((1, cells), jnp.int32),
            pltpu.VMEM((1, elements), jnp.int32),
            pltpu.VMEM(focal_delay.shape, jnp.float32),
            pltpu.VMEM(flaw_size.shape, jnp.float32),
            pltpu.VMEM(flaw_slope.shape, jnp.float32),
            pltpu.VMEM((2, 2 * freq_total, 2 * freq_total), jnp.bfloat16),
            pltpu.VMEM((2, HALF, 2 * elements, cells), jnp.bfloat16),
            pltpu.VMEM((cells, cells), jnp.bfloat16),
            pltpu.VMEM((4 * FG, elements), jnp.float32),
            pltpu.VMEM((2 * FG, elements), jnp.float32),
            pltpu.VMEM((2, 4 * FG, elements), jnp.float32),
            pltpu.VMEM((2, 4 * FG, elements), jnp.float32),
            pltpu.VMEM((rows, FG), jnp.float32),
            pltpu.VMEM((rows, FG), jnp.bfloat16),
            pltpu.VMEM((2, rows, FG), jnp.bfloat16),
            pltpu.VMEM((2, rows, FG), jnp.bfloat16),
            pltpu.VMEM((2, rows, FG), jnp.bfloat16),
            pltpu.VMEM((2, freq_count, chunk, FG), jnp.bfloat16),
            pltpu.VMEM((columns // 2, 2 * freq_total, 2 * FG), jnp.float32),
            pltpu.VMEM((FG, FG), jnp.float32),
            pltpu.SemaphoreType.DMA((7,)),
            pltpu.SemaphoreType.DMA((2,)),
            pltpu.SemaphoreType.DMA((2,)),
            pltpu.SemaphoreType.DMA((2,)),
            pltpu.SemaphoreType.DMA((2, freq_count)),
            pltpu.SemaphoreType.DMA((2, freq_count)),
        ],
        compiler_params=pltpu.CompilerParams(
            collective_id=0, has_side_effects=True, vmem_limit_bytes=67_043_328
        ),
    )(
        flaw_blocks,
        flaw_cells.reshape(1, cells),
        element_channel.reshape(1, elements),
        focal_delay,
        beam_field.reshape(HALF, 2, 2 * elements, cells),
        flaw_size,
        flaw_slope,
        jnp.asarray(half_twiddles(freq_count)),
    )
    flaw_peak = jnp.sqrt(power[:, :columns]) * (1.0 / math.sqrt(freq_total))
    detection = jax.nn.sigmoid(STEEP * (jnp.log(flaw_peak + EPS) - jnp.log(noise_level)))
    return (flaw_peak, detection)


def plain_body(
    flaw_cells,
    flaw_blocks,
    element_channel,
    focal_delay,
    beam_field,
    flaw_size,
    flaw_slope,
    noise_level,
):
    freq_count = lax.axis_size("freq")
    freq_total = W_DEV * freq_count
    group_total = flaw_size.shape[0]
    row_total = NB * SB
    first_freq = lax.axis_index("freq") * W_DEV
    angular = (first_freq + jnp.arange(W_DEV, dtype=jnp.int32)).astype(jnp.float32) * (
        math.pi / freq_total
    )
    scan_rows = (
        flaw_blocks.reshape(group_total, NB)[:, :, None] * SB
        + jnp.arange(SB, dtype=jnp.int32)[None, None, :]
    ).reshape(group_total, row_total)
    delays = jnp.moveaxis(
        jnp.take(jnp.take(focal_delay, element_channel, axis=0), scan_rows, axis=1), 0, 2
    )
    fields = jnp.take(beam_field, flaw_cells, axis=3).reshape(
        W_DEV, 2, element_channel.shape[0], group_total, FG
    )
    k_real, k_imag = kirchhoff(angular, flaw_size, flaw_slope)
    focal_terms = focal_law(angular, delays)
    field_terms = field_matrix(fields)
    product = jnp.einsum(
        "wgre,wegf->gwrf", focal_terms, field_terms, preferred_element_type=jnp.float32
    )
    partial_value = combine(product, k_real, k_imag).astype(jnp.bfloat16)
    rounded_term = lax.optimization_barrier(partial_value).astype(jnp.float32)
    summed = lax.psum_scatter(
        rounded_term.astype(jnp.bfloat16), "elem", scatter_dimension=0, tiled=True
    )
    partial_peak = regroup_peaks(
        lax.all_to_all(summed, "freq", split_axis=3, concat_axis=1, tiled=True)
    )
    whole_peak = lax.pmax(partial_peak, "freq")
    columns = FG // freq_count
    flaw_peak = lax.dynamic_slice_in_dim(whole_peak, lax.axis_index("freq") * columns, columns, 1)
    detection = jax.nn.sigmoid(STEEP * (jnp.log(flaw_peak + EPS) - jnp.log(noise_level)))
    return (flaw_peak, detection)


def solution(mesh):
    in_specs = (
        P("batch"),
        P("batch"),
        P("elem"),
        P(),
        P("freq", None, "elem", None),
        P("batch", None),
        P("batch", None),
        P(("batch", "elem"), "freq"),
    )
    out_specs = (P(("batch", "elem"), "freq"), P(("batch", "elem"), "freq"))
    freq_count = mesh.shape["freq"]
    freq_total = W_DEV * freq_count
    whole_tiles = FG % (2 * freq_count) == 0 and freq_total % FG == 0
    body = fused_body if whole_tiles and 2 * freq_total <= T_CAP else plain_body
    return jax.shard_map(body, mesh=mesh, in_specs=in_specs, out_specs=out_specs, check_vma=False)
```

```python
import functools
import math

import jax
import jax.numpy as jnp
import numpy as np
from jax import lax
from jax.experimental import pallas as pl
from jax.experimental.pallas import tpu as pltpu
from jax.sharding import PartitionSpec as P

W_DEV = 16
FG = 128
NB = 4
SB = 32
T_CAP = 1024


EDGE = 0.6
STEEP = 3.0
EPS = 1e-05


def kirchhoff(angular, flaw_size, flaw_slope):
    angles = angular[None, :, None] * (2.0 * flaw_size * flaw_slope)[:, None, :]
    real_part = flaw_size[:, None, :] * (1.0 + EDGE) * jnp.cos(angles)
    imag_part = flaw_size[:, None, :] * (EDGE - 1.0) * jnp.sin(angles)
    return (real_part, imag_part)


def focal_law(angular, delays):
    phases = angular[:, None, None, None] * delays[None]
    return jnp.concatenate([jnp.cos(phases), -jnp.sin(phases)], axis=-1).astype(jnp.bfloat16)


def field_matrix(fields):
    real_part = fields[:, 0]
    imag_part = fields[:, 1]
    upper_rows = jnp.concatenate([real_part, imag_part], axis=-1)
    lower_rows = jnp.concatenate([-imag_part, real_part], axis=-1)
    return jnp.concatenate([upper_rows, lower_rows], axis=1)


def combine(product, k_real, k_imag):
    columns = k_real.shape[-1]
    real_part = product[..., :columns]
    imag_part = product[..., columns:]
    scale_real = k_real[:, :, None, :]
    scale_imag = k_imag[:, :, None, :]
    return jnp.stack(
        [
            scale_real * real_part - scale_imag * imag_part,
            scale_real * imag_part + scale_imag * real_part,
        ],
        axis=2,
    )


def envelope_peak(spectra, row_count):
    groups, freq_total, planes, columns = spectra.shape
    sample_count = min(T_CAP, 2 * freq_total)
    time_block = min(128, sample_count)
    freq_index = jnp.arange(freq_total, dtype=jnp.int32)
    scaling = 1.0 / math.sqrt(freq_total)

    def advance(step_index, running):
        sample_times = step_index * time_block + jnp.arange(time_block, dtype=jnp.int32)
        phase_steps = freq_index[:, None] * sample_times[None, :] % (2 * freq_total)
        angles = phase_steps.astype(jnp.float32) * (math.pi / freq_total)
        cosine = jnp.cos(angles)
        sine_part = jnp.sin(angles)
        twiddle = jnp.stack(
            [jnp.stack([cosine, sine_part], axis=1), jnp.stack([-sine_part, cosine], axis=1)],
            axis=1,
        )
        twiddle_high = lax.optimization_barrier(twiddle.astype(jnp.bfloat16))
        twiddle_low = (twiddle - twiddle_high.astype(jnp.float32)).astype(jnp.bfloat16)
        signal = jnp.einsum(
            "gwcx,wckt->gkxt", spectra, twiddle_high, preferred_element_type=jnp.float32
        )
        signal = signal + jnp.einsum(
            "gwcx,wckt->gkxt", spectra, twiddle_low, preferred_element_type=jnp.float32
        )
        signal = signal * scaling
        magnitude = jnp.sqrt(signal[:, 0] * signal[:, 0] + signal[:, 1] * signal[:, 1])
        magnitude = magnitude.reshape(groups, row_count, columns // row_count, time_block)
        return jnp.maximum(running, jnp.max(magnitude, axis=(1, 3)))

    initial = jnp.zeros((groups, columns // row_count), jnp.float32)
    return lax.fori_loop(0, sample_count // time_block, advance, initial)


def regroup_peaks(moved):
    groups, freq_total, planes, row_count, flaw_count = moved.shape
    return envelope_peak(
        moved.reshape(groups, freq_total, planes, row_count * flaw_count), row_count
    )


MESH = pl.DeviceIdType.MESH
HALF = W_DEV // 2
TILE_ROWS = 2 * HALF
NT_DIMS = (((1,), (1,)), ((), ()))


def dot_rows(left, right):
    return lax.dot_general(left, right, NT_DIMS, preferred_element_type=jnp.float32)


def unit_phasor(turns):
    rest = turns - jnp.floor(turns + 0.5)
    angle = rest * math.pi
    square = angle * angle
    sine = jnp.full_like(angle, -1.0 / math.factorial(11))
    for order, sign in ((9, 1.0), (7, -1.0), (5, 1.0), (3, -1.0), (1, 1.0)):
        sine = sine * square + sign / math.factorial(order)
    sine = sine * angle
    cosine = jnp.full_like(angle, 1.0 / math.factorial(12))
    for order, sign in ((10, -1.0), (8, 1.0), (6, -1.0), (4, 1.0), (2, -1.0), (0, 1.0)):
        cosine = cosine * square + sign / math.factorial(order)
    return 1.0 - 2.0 * sine * sine, -2.0 * sine * cosine


def half_twiddles(freq_count):
    freq_total = W_DEV * freq_count
    samples = np.arange(freq_total)
    halves = []
    for parity in range(2):
        freqs = (np.arange(freq_count)[:, None] * W_DEV + 2 * np.arange(HALF)[None, :] + parity).reshape(-1)
        angles = (samples[:, None] * freqs[None, :] % (2 * freq_total)) * (np.pi / freq_total)
        cosine, sine = np.cos(angles), np.sin(angles)
        real_rows = np.stack([cosine, -sine], axis=-1).reshape(freq_total, -1)
        imag_rows = np.stack([sine, cosine], axis=-1).reshape(freq_total, -1)
        whole = np.concatenate([real_rows, imag_rows], axis=0).astype(np.float32)
        high = whole.astype(jnp.bfloat16)
        low = (whole - high.astype(np.float32)).astype(jnp.bfloat16)
        halves.append(np.concatenate([high, low], axis=1))
    return np.stack(halves)


def inspect_kernel(
    freq_count,
    blocks_hbm,
    cells_hbm,
    channel_hbm,
    delay_hbm,
    field_hbm,
    size_hbm,
    slope_hbm,
    twiddle_hbm,
    power_ref,
    blocks_ref,
    cells_ref,
    channel_ref,
    delay_ref,
    size_ref,
    slope_ref,
    twiddle_ref,
    field_ref,
    select_ref,
    theta_ref,
    amp_ref,
    phase_ref,
    turn_ref,
    stage_ref,
    own_ref,
    give_ref,
    take_ref,
    spec_ref,
    recv_ref,
    even_ref,
    top_ref,
    load_sem,
    field_sem,
    give_sem,
    take_sem,
    send_sem,
    recv_sem,
):
    freq_total = W_DEV * freq_count
    columns = FG // freq_count
    chunk = columns * TILE_ROWS
    me = lax.axis_index("freq")
    mine = lax.axis_index("elem")
    sibling = 1 - mine

    small = [
        pltpu.make_async_copy(source, target, load_sem.at[index])
        for index, (source, target) in enumerate(
            (
                (cells_hbm, cells_ref),
                (channel_hbm, channel_ref),
                (blocks_hbm, blocks_ref),
                (delay_hbm, delay_ref),
                (size_hbm, size_ref),
                (slope_hbm, slope_ref),
                (twiddle_hbm, twiddle_ref),
            )
        )
    ]
    for load in small[:-1]:
        load.start()
    loads = [
        pltpu.make_async_copy(field_hbm.at[:, parity], field_ref.at[parity], field_sem.at[parity])
        for parity in range(2)
    ]
    for load in loads:
        load.start()
    small[-1].start()

    barrier = pltpu.get_barrier_semaphore()
    pl.semaphore_signal(barrier, inc=1, device_id={"elem": sibling}, device_id_type=MESH)
    for step in range(1, freq_count):
        pl.semaphore_signal(
            barrier, inc=1, device_id={"freq": lax.rem(me + step, freq_count)}, device_id_type=MESH
        )

    small[0].wait()
    cell_count = cells_ref.shape[1]
    cell_rows = lax.broadcasted_iota(jnp.int32, (cell_count, cell_count), 0)
    chosen = jnp.where(cell_rows == cells_ref[...], 1.0, 0.0)
    select_ref[...] = jnp.transpose(chosen).astype(jnp.bfloat16)

    for load in small[1:-1]:
        load.wait()
    channel_count, scan_count = delay_ref.shape
    element_count = channel_ref.shape[1]
    channel_rows = lax.broadcasted_iota(jnp.int32, (channel_count, element_count), 0)
    drives = jnp.transpose(jnp.where(channel_rows == channel_ref[...], 1.0, 0.0)).astype(jnp.bfloat16)
    sub = lax.broadcasted_iota(jnp.int32, (SB, scan_count), 0)
    lane = lax.broadcasted_iota(jnp.int32, (SB, scan_count), 1)
    rows = jnp.concatenate(
        [jnp.where(lane == sub + blocks_ref[j] * SB, 1.0, 0.0) for j in range(2 * NB)], axis=0
    ).astype(jnp.bfloat16)
    rest = delay_ref[...]
    delays = jnp.zeros((2 * FG, element_count), jnp.float32)
    for _ in range(3):
        piece = rest.astype(jnp.bfloat16)
        rest = rest - piece.astype(jnp.float32)
        by_element = jnp.dot(drives, piece, preferred_element_type=jnp.float32).astype(jnp.bfloat16)
        delays = delays + dot_rows(rows, by_element)
    theta_ref[: 2 * FG] = delays
    for group in range(2):
        size = jnp.transpose(jnp.broadcast_to(size_ref[group : group + 1, :], (FG, FG)))
        slope = jnp.transpose(jnp.broadcast_to(slope_ref[group : group + 1, :], (FG, FG)))
        theta_ref[(2 + group) * FG : (3 + group) * FG] = 2.0 * size * slope
        amp_ref[group * FG : (group + 1) * FG] = size
    scale = 0.5 / freq_total
    turn_real, turn_imag = unit_phasor(theta_ref[...] * (2.0 * scale))
    turn_ref[0] = turn_real
    turn_ref[1] = turn_imag

    def group_spectra(parity, group, first, count):
        base = pl.multiple_of(group * FG, FG)
        flaws = pl.multiple_of(group * FG + first, count)
        tail = pl.multiple_of((2 + group) * FG + first, count)

        def one_freq(index, carry):
            focal_real = phase_ref[0, pl.ds(base, FG), :]
            focal_imag = phase_ref[1, pl.ds(base, FG), :]
            fields = dot_rows(select_ref[pl.ds(flaws, count), :], field_ref[parity, index])
            weights = jnp.concatenate(
                [
                    jnp.concatenate([focal_real, -focal_imag], axis=1),
                    jnp.concatenate([focal_imag, focal_real], axis=1),
                ],
                axis=0,
            ).astype(jnp.bfloat16)
            product = dot_rows(fields.astype(jnp.bfloat16), weights)
            real_part = product[:, :FG]
            imag_part = product[:, FG:]
            edge_real = phase_ref[0, pl.ds(tail, count), :]
            edge_imag = phase_ref[1, pl.ds(tail, count), :]
            amp = amp_ref[pl.ds(flaws, count), :]
            k_real = amp * (1.0 + EDGE) * edge_real
            k_imag = amp * (1.0 - EDGE) * edge_imag
            stage_ref[pl.ds(2 * index, count, stride=TILE_ROWS), :] = k_real * real_part - k_imag * imag_part
            stage_ref[pl.ds(2 * index + 1, count, stride=TILE_ROWS), :] = k_real * imag_part + k_imag * real_part
            for start, size, old_real, old_imag in (
                (base, FG, focal_real, focal_imag),
                (tail, count, edge_real, edge_imag),
            ):
                step_real = turn_ref[0, pl.ds(start, size), :]
                step_imag = turn_ref[1, pl.ds(start, size), :]
                phase_ref[0, pl.ds(start, size), :] = old_real * step_real - old_imag * step_imag
                phase_ref[1, pl.ds(start, size), :] = old_real * step_imag + old_imag * step_real
            return carry

        lax.fori_loop(0, HALF, one_freq, 0, unroll=2)

    half_count = freq_count // 2
    side = me // half_count
    peers = [(1 - side) * half_count + lax.rem(me + step, half_count) for step in range(half_count)]
    peers += [side * half_count + lax.rem(me + step, half_count) for step in range(1, half_count)]
    far = list(enumerate(peers))[:half_count]
    near = list(enumerate(peers))[half_count:]
    half_flaws = FG // 2
    pieces = (
        (0, (1 - side) * half_flaws, half_flaws, far, False),
        (0, side * half_flaws, half_flaws, near, True),
        (1, 0, FG, far + near, True),
    )
    pass_copies = []
    sends = []
    for piece, (parity, first, count, targets, keeps) in enumerate(pieces):
        size = count * TILE_ROWS
        span = pl.ds(pl.multiple_of(first * TILE_ROWS, size), size)
        freq_scale = (me * W_DEV + parity).astype(jnp.float32) * scale
        start_real, start_imag = unit_phasor(theta_ref[...] * freq_scale)
        phase_ref[0] = start_real
        phase_ref[1] = start_imag
        if piece != 1:
            loads[parity].wait()
        group_spectra(parity, sibling, first, count)
        give_ref[parity, span, :] = stage_ref[:size].astype(jnp.bfloat16)
        if piece == 0:
            pl.semaphore_wait(barrier, freq_count)
        swap = pltpu.make_async_remote_copy(
            src_ref=give_ref.at[parity, span],
            dst_ref=take_ref.at[parity, span],
            send_sem=give_sem.at[piece],
            recv_sem=take_sem.at[piece],
            device_id={"elem": sibling},
            device_id_type=MESH,
        )
        swap.start()
        pass_copies.append(swap)
        group_spectra(parity, mine, first, count)
        own_ref[:size] = stage_ref[:size].astype(jnp.bfloat16)
        swap.wait_recv()
        total = own_ref[:size].astype(jnp.float32) + take_ref[parity, span, :].astype(jnp.float32)
        spec_ref[parity, span, :] = total.astype(jnp.bfloat16)
        for step, peer in targets:
            copy = pltpu.make_async_remote_copy(
                src_ref=spec_ref.at[parity, pl.ds(pl.multiple_of(peer * chunk, chunk), chunk)],
                dst_ref=recv_ref.at[parity, me],
                send_sem=send_sem.at[parity, step],
                recv_sem=recv_sem.at[parity, me],
                device_id={"freq": peer},
                device_id_type=MESH,
            )
            copy.start()
            sends.append(copy)
        if keeps:
            recv_ref[parity, me] = spec_ref[parity, pl.ds(pl.multiple_of(me * chunk, chunk), chunk), :]

    def await_half(parity):
        for step, source in enumerate(peers):
            pltpu.make_async_remote_copy(
                src_ref=spec_ref.at[parity, pl.ds(0, chunk)],
                dst_ref=recv_ref.at[parity, source],
                send_sem=send_sem.at[parity, step],
                recv_sem=recv_sem.at[parity, source],
                device_id={"freq": source},
                device_id_type=MESH,
            ).wait_recv()

    def half_signal(parity, pair):
        sides = [
            recv_ref[parity, :, pl.ds(pl.multiple_of((2 * pair + side) * TILE_ROWS, TILE_ROWS), TILE_ROWS), :].reshape(
                freq_total, FG
            )
            for side in range(2)
        ]
        both = jnp.concatenate(sides, axis=1)
        return jnp.dot(
            twiddle_ref[parity], jnp.concatenate([both, both], axis=0), preferred_element_type=jnp.float32
        )

    small[-1].wait()
    await_half(0)

    def even_pair(pair, carry):
        even_ref[pair] = half_signal(0, pair)
        return carry

    lax.fori_loop(0, columns // 2, even_pair, 0)
    top_ref[...] = jnp.zeros_like(top_ref)
    await_half(1)

    def odd_pair(pair, carry):
        odd = half_signal(1, pair)
        even = even_ref[pair]
        first = even + odd
        second = even - odd
        power = jnp.maximum(
            first[:freq_total] * first[:freq_total] + first[freq_total:] * first[freq_total:],
            second[:freq_total] * second[:freq_total] + second[freq_total:] * second[freq_total:],
        )
        best = jnp.max(power, axis=0, keepdims=True)
        top_ref[pl.ds(2 * pair, 1), :] = best[:, :FG]
        top_ref[pl.ds(2 * pair + 1, 1), :] = best[:, FG:]
        return carry

    lax.fori_loop(0, columns // 2, odd_pair, 0, unroll=4 if columns % 8 == 0 else 1)
    power_ref[...] = jnp.max(jnp.transpose(top_ref[...]), axis=0, keepdims=True)
    for copy in pass_copies:
        copy.wait_send()
    for copy in sends:
        copy.wait_send()


def fused_body(
    flaw_cells,
    flaw_blocks,
    element_channel,
    focal_delay,
    beam_field,
    flaw_size,
    flaw_slope,
    noise_level,
):
    freq_count = lax.axis_size("freq")
    columns = FG // freq_count
    elements, cells = beam_field.shape[2:]
    vmem = pl.BlockSpec(memory_space=pltpu.VMEM)
    rows = FG * TILE_ROWS
    chunk = columns * TILE_ROWS
    freq_total = W_DEV * freq_count
    hbm = pl.BlockSpec(memory_space=pltpu.MemorySpace.HBM)
    power = pl.pallas_call(
        functools.partial(inspect_kernel, freq_count),
        out_shape=jax.ShapeDtypeStruct((1, FG), jnp.float32),
        in_specs=[hbm] * 8,
        out_specs=vmem,
        scratch_shapes=[
            pltpu.SMEM(flaw_blocks.shape, jnp.int32),
            pltpu.VMEM((1, cells), jnp.int32),
            pltpu.VMEM((1, elements), jnp.int32),
            pltpu.VMEM(focal_delay.shape, jnp.float32),
            pltpu.VMEM(flaw_size.shape, jnp.float32),
            pltpu.VMEM(flaw_slope.shape, jnp.float32),
            pltpu.VMEM((2, 2 * freq_total, 2 * freq_total), jnp.bfloat16),
            pltpu.VMEM((2, HALF, 2 * elements, cells), jnp.bfloat16),
            pltpu.VMEM((cells, cells), jnp.bfloat16),
            pltpu.VMEM((4 * FG, elements), jnp.float32),
            pltpu.VMEM((2 * FG, elements), jnp.float32),
            pltpu.VMEM((2, 4 * FG, elements), jnp.float32),
            pltpu.VMEM((2, 4 * FG, elements), jnp.float32),
            pltpu.VMEM((rows, FG), jnp.float32),
            pltpu.VMEM((rows, FG), jnp.bfloat16),
            pltpu.VMEM((2, rows, FG), jnp.bfloat16),
            pltpu.VMEM((2, rows, FG), jnp.bfloat16),
            pltpu.VMEM((2, rows, FG), jnp.bfloat16),
            pltpu.VMEM((2, freq_count, chunk, FG), jnp.bfloat16),
            pltpu.VMEM((columns // 2, 2 * freq_total, 2 * FG), jnp.float32),
            pltpu.VMEM((FG, FG), jnp.float32),
            pltpu.SemaphoreType.DMA((7,)),
            pltpu.SemaphoreType.DMA((2,)),
            pltpu.SemaphoreType.DMA((3,)),
            pltpu.SemaphoreType.DMA((3,)),
            pltpu.SemaphoreType.DMA((2, freq_count)),
            pltpu.SemaphoreType.DMA((2, freq_count)),
        ],
        compiler_params=pltpu.CompilerParams(
            collective_id=0, has_side_effects=True, vmem_limit_bytes=67_043_328
        ),
    )(
        flaw_blocks,
        flaw_cells.reshape(1, cells),
        element_channel.reshape(1, elements),
        focal_delay,
        beam_field.reshape(HALF, 2, 2 * elements, cells),
        flaw_size,
        flaw_slope,
        jnp.asarray(half_twiddles(freq_count)),
    )
    flaw_peak = jnp.sqrt(power[:, :columns]) * (1.0 / math.sqrt(freq_total))
    detection = jax.nn.sigmoid(STEEP * (jnp.log(flaw_peak + EPS) - jnp.log(noise_level)))
    return (flaw_peak, detection)


def plain_body(
    flaw_cells,
    flaw_blocks,
    element_channel,
    focal_delay,
    beam_field,
    flaw_size,
    flaw_slope,
    noise_level,
):
    freq_count = lax.axis_size("freq")
    freq_total = W_DEV * freq_count
    group_total = flaw_size.shape[0]
    row_total = NB * SB
    first_freq = lax.axis_index("freq") * W_DEV
    angular = (first_freq + jnp.arange(W_DEV, dtype=jnp.int32)).astype(jnp.float32) * (
        math.pi / freq_total
    )
    scan_rows = (
        flaw_blocks.reshape(group_total, NB)[:, :, None] * SB
        + jnp.arange(SB, dtype=jnp.int32)[None, None, :]
    ).reshape(group_total, row_total)
    delays = jnp.moveaxis(
        jnp.take(jnp.take(focal_delay, element_channel, axis=0), scan_rows, axis=1), 0, 2
    )
    fields = jnp.take(beam_field, flaw_cells, axis=3).reshape(
        W_DEV, 2, element_channel.shape[0], group_total, FG
    )
    k_real, k_imag = kirchhoff(angular, flaw_size, flaw_slope)
    focal_terms = focal_law(angular, delays)
    field_terms = field_matrix(fields)
    product = jnp.einsum(
        "wgre,wegf->gwrf", focal_terms, field_terms, preferred_element_type=jnp.float32
    )
    partial_value = combine(product, k_real, k_imag).astype(jnp.bfloat16)
    rounded_term = lax.optimization_barrier(partial_value).astype(jnp.float32)
    summed = lax.psum_scatter(
        rounded_term.astype(jnp.bfloat16), "elem", scatter_dimension=0, tiled=True
    )
    partial_peak = regroup_peaks(
        lax.all_to_all(summed, "freq", split_axis=3, concat_axis=1, tiled=True)
    )
    whole_peak = lax.pmax(partial_peak, "freq")
    columns = FG // freq_count
    flaw_peak = lax.dynamic_slice_in_dim(whole_peak, lax.axis_index("freq") * columns, columns, 1)
    detection = jax.nn.sigmoid(STEEP * (jnp.log(flaw_peak + EPS) - jnp.log(noise_level)))
    return (flaw_peak, detection)


def solution(mesh):
    in_specs = (
        P("batch"),
        P("batch"),
        P("elem"),
        P(),
        P("freq", None, "elem", None),
        P("batch", None),
        P("batch", None),
        P(("batch", "elem"), "freq"),
    )
    out_specs = (P(("batch", "elem"), "freq"), P(("batch", "elem"), "freq"))
    freq_count = mesh.shape["freq"]
    freq_total = W_DEV * freq_count
    whole_tiles = FG % (2 * freq_count) == 0 and freq_total % FG == 0
    body = fused_body if whole_tiles and 2 * freq_total <= T_CAP else plain_body
    return jax.shard_map(body, mesh=mesh, in_specs=in_specs, out_specs=out_specs, check_vma=False)
```
